32 devices in a mesh: region: 32 (over z, y, x, core).
Axes of the slice: x: 2, y: 2, z: 4, core: 2. Of those that a mesh axis runs over, the one named last changes fastest.
Arguments:
- gaussians: float32 [32, 9, 4096], P('region')
- depth: int32 [32, 512, 8], P('region'), may hold values from 0 to 7, each once within a row
- coverage: int32 [32, 512], P('region'), may hold values 0 or 1
- flips: int32 [512, 31], replicated, may hold values 0 or 1
- features: bfloat16 [131072, 384], P('region'), may hold values from -6 to 6
- w_first: bfloat16 [384, 384], replicated, may hold values from -0.3125 to 0.3125
- b_first: float32 [384], replicated, may hold values from -3 to 3
- w_second: bfloat16 [384], replicated, may hold values from -0.3125 to 0.3125
- target: float32 [3, 131072], P(None, 'region'), may hold values from 0 to 1
Outputs:
- pixel_loss: float32 [131072], P('region')
- splat_grads: float32 [32, 9, 4096], P('region')
The draws below stay inside these ranges and needn't reach their ends.
Inputs may be any that keep to these rules, and one draw needn't show every extreme that they name: Each tile's 8 depth ranks of one region are a permutation of 0 to 7.
All inputs are finite; a program needn't handle non-finite values. No bound on the sum of `coverage` on one device may be relied on, other than what follows from the above.
Results may differ from the reference program's by a relative error of at most 0.0022.
Values sent between devices are 32-bit elements; how exact they have to be, the bound alone decides.
A program may use at most 64 MiB of HBM per device.

```python
import math
import jax
import jax.numpy as jnp
from jax import lax

TILES = 512
TSIDE = 16
GPT = 8
FEAT = 384
HID = 384
REGIONS = 32
NODES = 31
PIXELS = 131072


def draw_gaussians(key, part):
    lower = jnp.array([-1.0, -1.0, 0.0, 0.0, -1.5, -4.0, -2.5, -2.5, -2.5], jnp.float32)
    upper = jnp.array([TSIDE + 1.0, TSIDE + 1.0, math.log(TSIDE * 0.5), math.log(TSIDE * 0.5), 1.5, 1.0, 2.5, 2.5, 2.5], jnp.float32)
    uniform_draw = jax.random.uniform(key, (REGIONS, 9, TILES * GPT), jnp.float32)
    return lower[None, :, None] + (upper - lower)[None, :, None] * uniform_draw


def with_ends(values, rng, smallest, high):
    index_at = [jax.random.randint(jax.random.fold_in(rng, axis), (), 0, length) for axis, length in enumerate(values.shape)]
    longest = values.shape.index(max(values.shape))
    next_to = index_at[:longest] + [(index_at[longest] + 1) % values.shape[longest]] + index_at[longest + 1:]
    return values.at[tuple(index_at)].set(smallest).at[tuple(next_to)].set(high)


def shard_levels(own_key, dims, cuts, smallest, high):
    def one(dim, parts):
        heights = jax.random.uniform(jax.random.fold_in(jax.random.fold_in(own_key, 6), dim), (parts,), jnp.float32, smallest / len(cuts), high / len(cuts))
        return jnp.repeat(jnp.exp(heights), dims[dim] // parts).reshape((-1,) + (1,) * (len(dims) - dim - 1))

    loudness = one(*cuts[0])
    for cut in cuts[1:]:
        loudness = loudness * one(*cut)
    return loudness


def normal_values(stream_key, dims, deviation, bound, split=(), dtype=jnp.bfloat16):
    entries = deviation * jax.random.normal(stream_key, dims, jnp.float32)
    if split:
        entries = entries * shard_levels(stream_key, dims, split, -0.22, 0.18)
    return jnp.clip(entries, -bound, bound).astype(dtype)


def setup_inputs(seed: int = 0) -> dict:
    key_list = jax.random.split(jax.random.key(seed), 10)
    gaussians = draw_gaussians(jax.random.fold_in(key_list[9], 71), 0)
    depth = jax.vmap(lambda own: jax.random.permutation(own, GPT))(jax.random.split(key_list[1], REGIONS * TILES)).reshape((REGIONS, TILES, GPT)).astype(jnp.int32)
    coverage = with_ends((jax.random.randint(key_list[2], (REGIONS, TILES), 0, 4) < 1).astype(jnp.int32), jax.random.fold_in(key_list[2], 1), 0, 1)
    flips = with_ends((jax.random.randint(key_list[3], (TILES, NODES), 0, 2) < 1).astype(jnp.int32), jax.random.fold_in(key_list[3], 1), 0, 1)
    features = normal_values(key_list[4], (PIXELS, FEAT), 1.0, 6.0, ((0, 32),))
    w_first = normal_values(key_list[5], (FEAT, HID), FEAT ** -0.5, 0.3125)
    b_first = normal_values(key_list[6], (HID,), 0.5, 3.0, (), jnp.float32)
    w_second = normal_values(key_list[7], (HID,), HID ** -0.5, 0.3125)
    target = jnp.clip(1.0 * jax.random.uniform(key_list[8], (3, PIXELS), jnp.float32) ** shard_levels(key_list[8], (3, PIXELS), ((1, 32),), -0.2, 0.2), 0.0, 1.0)
    return {"gaussians": gaussians, "depth": depth, "coverage": coverage, "flips": flips, "features": features, "w_first": w_first, "b_first": b_first, "w_second": w_second, "target": target}


def render_tiles(params, splat_ranks, covered):
    pixel_index = jnp.arange(TSIDE * TSIDE)
    column_pos = (pixel_index % TSIDE).astype(jnp.float32) + 0.5
    row_pos = (pixel_index // TSIDE).astype(jnp.float32) + 0.5
    delta_x = column_pos[None, None, :] - params[0][:, :, None]
    delta_y = row_pos[None, None, :] - params[1][:, :, None]
    unit_x = delta_x * jnp.exp(-params[2])[:, :, None]
    unit_y = delta_y * jnp.exp(-params[3])[:, :, None]
    correlation = (0.9 * jnp.tanh(params[4]))[:, :, None]
    quadratic = (unit_x * unit_x - 2.0 * correlation * unit_x * unit_y + unit_y * unit_y) / (1.0 - correlation * correlation)
    opacity = 0.99 * jax.nn.sigmoid(params[5]) * covered[:, None].astype(jnp.float32)
    absorb = opacity[:, :, None] * jnp.exp(-0.5 * quadratic)
    log_trans = jnp.log1p(-absorb)
    prior = (splat_ranks[:, None, :] < splat_ranks[:, :, None]).astype(jnp.float32)
    leading = jnp.einsum('tgh,thp->tgp', prior, log_trans, precision=lax.Precision.HIGHEST)
    weight = jnp.exp(leading) * absorb
    colors = jax.nn.sigmoid(params[6:9])
    color_sum = lax.optimization_barrier(jnp.sum(colors[:, :, :, None] * weight[None], 2))
    transmit = jnp.exp(lax.optimization_barrier(jnp.sum(log_trans, axis=1)))
    return jnp.concatenate([color_sum, transmit[None]], 0)

def over_pair(front_layer, back_layer):
    blended = front_layer[:, :3] + front_layer[:, 3:4] * back_layer[:, :3]
    transmit = front_layer[:, 3:4] * back_layer[:, 3:4]
    return jnp.concatenate([blended, transmit], 1)

def tree_levels(stack, stripe_flips):
    number = stack.shape[0]
    while number > 1:
        half_count = number // 2
        in_front = (stripe_flips[:, half_count - 1:2 * half_count - 1].T > 0)[:, None, :, None]
        paired = stack.reshape((half_count, 2) + stack.shape[1:])
        front_layer = jnp.where(in_front, paired[:, 1], paired[:, 0])
        back_layer = jnp.where(in_front, paired[:, 0], paired[:, 1])
        stack = over_pair(front_layer, back_layer)
        number = half_count
    return stack[0]

def uncertainty(stripe_feats, w_first, b_first, w_second):
    hidden = jax.nn.gelu(jnp.dot(stripe_feats, w_first, preferred_element_type=jnp.float32) + b_first).astype(jnp.bfloat16)
    return 0.5 + jax.nn.softplus(jnp.dot(hidden, w_second, preferred_element_type=jnp.float32))

def reference(gaussians, depth, coverage, flips, features, w_first, b_first, w_second, target):
    regions = gaussians.shape[0]
    tile_count = depth.shape[1]
    splats = depth.shape[2]
    stripe_tiles = tile_count // regions
    tile_pixels = TSIDE * TSIDE
    grid_params = gaussians.reshape(regions, 9, tile_count, splats)

    def stripe_work(stripe_index):
        first_tile = (stripe_index * stripe_tiles).astype(jnp.int32)
        params = lax.dynamic_slice_in_dim(grid_params, first_tile, stripe_tiles, 2)
        splat_ranks = lax.dynamic_slice_in_dim(depth, first_tile, stripe_tiles, 1)
        covered = lax.dynamic_slice_in_dim(coverage, first_tile, stripe_tiles, 1)
        stripe_flips = lax.dynamic_slice_in_dim(flips, first_tile, stripe_tiles, 0)
        first_pixel = (first_tile * tile_pixels).astype(jnp.int32)
        stripe_feats = lax.dynamic_slice_in_dim(features, first_pixel, stripe_tiles * tile_pixels, 0)
        wanted = lax.dynamic_slice_in_dim(target, first_pixel, stripe_tiles * tile_pixels, 1).reshape(3, stripe_tiles, tile_pixels)
        spread = uncertainty(stripe_feats, w_first, b_first, w_second).reshape(stripe_tiles, tile_pixels)

        def stripe_loss(region_params):
            pieces = jax.vmap(render_tiles)(region_params, splat_ranks, covered)
            composite = tree_levels(pieces, stripe_flips)
            residual = composite[:3] + composite[3:4] - wanted
            return lax.optimization_barrier(jnp.sum(residual * residual, 0)) / (2.0 * spread * spread)
        loss_part, pull_back = jax.vjp(stripe_loss, params)
        gradient, = pull_back(jnp.ones_like(loss_part))
        return (loss_part + jnp.log(spread), gradient)
    losses, gradients = lax.map(stripe_work, jnp.arange(regions).astype(jnp.int32))
    pixel_loss = losses.reshape(tile_count * tile_pixels)
    splat_grads = gradients.transpose(1, 2, 0, 3, 4).reshape(regions, 9, tile_count * splats)
    return (pixel_loss, splat_grads)
```

```python
import functools

import jax
import jax.numpy as jnp
from jax import lax
from jax.experimental import pallas as pl
from jax.experimental.pallas import tpu as pltpu
from jax.sharding import PartitionSpec as P

TSIDE = 16
LANES = 128
NPAR = 10
LOG2E = 1.4426950408889634
HI = lax.Precision.HIGHEST


def render_kernel(
    x_ref, flip_ref, wanted_ref, spread_ref, loss_ref, grad_ref,
    d_ref, ex_ref, a_ref, t_ref, tree_ref, gtree_ref, mbuf, red_ref,
):
    regions, group = x_ref.shape[1:]
    splats = 8
    rows = wanted_ref.shape[1]
    nv = rows // 8
    stripe_tiles = group // splats
    span = LANES // stripe_tiles
    inner = regions - 1

    sub = lax.broadcasted_iota(jnp.int32, (8, LANES), 0)
    lane = lax.broadcasted_iota(jnp.int32, (8, LANES), 1)
    pix = sub * span + (lane & (span - 1))
    xpos = (pix & (TSIDE - 1)).astype(jnp.float32) + 0.5
    ypos = [((pix + 8 * v * span) // TSIDE).astype(jnp.float32) + 0.5 for v in range(nv)]
    vs = [slice(8 * v, 8 * v + 8) for v in range(nv)]

    spread_in = (
        lax.broadcasted_iota(jnp.int32, (group, LANES), 0) // splats
        == lax.broadcasted_iota(jnp.int32, (group, LANES), 1) // span
    ).astype(jnp.float32)
    gather_out = (
        lax.broadcasted_iota(jnp.int32, (LANES, group), 0) // span
        == lax.broadcasted_iota(jnp.int32, (LANES, group), 1) // splats
    ).astype(jnp.float32)
    rank_row = lax.broadcasted_iota(jnp.int32, (splats, group), 0).astype(jnp.float32)

    rho = 0.9 * jnp.tanh(x_ref[4])
    norm = lax.rsqrt(1.0 - rho * rho)
    d_ref[0] = x_ref[0]
    d_ref[1] = x_ref[1]
    d_ref[2] = jnp.exp(-x_ref[2])
    d_ref[3] = jnp.exp(-x_ref[3])
    d_ref[4] = norm
    d_ref[5] = rho * norm
    d_ref[6] = 0.99 * jax.nn.sigmoid(x_ref[5]) * x_ref[10]
    for k in range(3):
        d_ref[7 + k] = jax.nn.sigmoid(x_ref[6 + k])

    def expand(r, carry):
        mask = x_ref[9, pl.ds(r, 1), :] == rank_row
        picked = [
            jnp.where(mask, jnp.broadcast_to(d_ref[p, pl.ds(r, 1), :], (splats, group)), 0.0)
            for p in range(NPAR)
        ]
        ex_ref[r] = jnp.dot(
            jnp.concatenate(picked, 0), spread_in, precision=HI, preferred_element_type=jnp.float32
        )
        return carry

    lax.fori_loop(0, regions, expand, 0, unroll=2)

    def row(r, p, s):
        return ex_ref[r, pl.ds(p * splats + s, 1), :]

    def forward(r, carry):
        trans = [jnp.ones((8, LANES), jnp.float32)] * nv
        color = [[jnp.zeros((8, LANES), jnp.float32)] * nv for _ in range(3)]
        for s in range(splats):
            u = (xpos - row(r, 0, s)) * row(r, 2, s)
            us = u * row(r, 4, s)
            m_y, inv_y, skew, op = row(r, 1, s), row(r, 3, s), row(r, 5, s), row(r, 6, s)
            ks = [row(r, 7 + k, s) for k in range(3)]
            for v in range(nv):
                w = (ypos[v] - m_y) * inv_y
                p = us - skew * w
                alpha = op * jnp.exp2((p * p + w * w) * (-0.5 * LOG2E))
                a_ref[r * splats + s, vs[v]] = alpha
                t_ref[r * splats + s, vs[v]] = trans[v]
                weight = trans[v] * alpha
                for k in range(3):
                    color[k][v] = color[k][v] + weight * ks[k]
                trans[v] = trans[v] * (1.0 - alpha)
        for v in range(nv):
            for k in range(3):
                tree_ref[inner + r, k, vs[v]] = color[k][v]
            tree_ref[inner + r, 3, vs[v]] = trans[v]
        return carry

    lax.fori_loop(0, regions, forward, 0)

    def merge(i, carry):
        n = inner - 1 - i
        flip = jnp.broadcast_to(flip_ref[n], (8, LANES)) > 0.0
        for v in range(nv):
            low = [tree_ref[2 * n + 1, k, vs[v]] for k in range(4)]
            high = [tree_ref[2 * n + 2, k, vs[v]] for k in range(4)]
            front = [jnp.where(flip, h, l) for l, h in zip(low, high)]
            back = [jnp.where(flip, l, h) for l, h in zip(low, high)]
            for k in range(3):
                tree_ref[n, k, vs[v]] = front[k] + front[3] * back[k]
            tree_ref[n, 3, vs[v]] = front[3] * back[3]
        return carry

    lax.fori_loop(0, inner, merge, 0)

    for v in range(nv):
        spread = spread_ref[vs[v]]
        inv_square = 1.0 / (spread * spread)
        clear = tree_ref[0, 3, vs[v]]
        residual = [tree_ref[0, k, vs[v]] + clear - wanted_ref[k, vs[v]] for k in range(3)]
        total = residual[0] * residual[0] + residual[1] * residual[1] + residual[2] * residual[2]
        loss_ref[vs[v]] = 0.5 * total * inv_square + jnp.log(spread)
        gs = [res * inv_square for res in residual]
        for k in range(3):
            gtree_ref[0, k, vs[v]] = gs[k]
        gtree_ref[0, 3, vs[v]] = gs[0] + gs[1] + gs[2]

    def split(n, carry):
        flip = jnp.broadcast_to(flip_ref[n], (8, LANES)) > 0.0
        for v in range(nv):
            low = [tree_ref[2 * n + 1, k, vs[v]] for k in range(4)]
            high = [tree_ref[2 * n + 2, k, vs[v]] for k in range(4)]
            g = [gtree_ref[n, k, vs[v]] for k in range(4)]
            front_t = jnp.where(flip, high[3], low[3])
            back = [jnp.where(flip, l, h) for l, h in zip(low, high)]
            g_front_t = g[0] * back[0] + g[1] * back[1] + g[2] * back[2] + g[3] * back[3]
            for k in range(4):
                g_front = g[k] if k < 3 else g_front_t
                g_back = front_t * g[k]
                gtree_ref[2 * n + 1, k, vs[v]] = jnp.where(flip, g_back, g_front)
                gtree_ref[2 * n + 2, k, vs[v]] = jnp.where(flip, g_front, g_back)
        return carry

    lax.fori_loop(0, inner, split, 0)

    def backward(r, carry):
        gs = [[gtree_ref[inner + r, k, vs[v]] for v in range(nv)] for k in range(3)]
        behind = [gtree_ref[inner + r, 3, vs[v]] for v in range(nv)]
        for s in reversed(range(splats)):
            u = (xpos - row(r, 0, s)) * row(r, 2, s)
            m_y, inv_y = row(r, 1, s), row(r, 3, s)
            ks = [row(r, 7 + k, s) for k in range(3)]
            acc = None
            for v in range(nv):
                alpha = a_ref[r * splats + s, vs[v]]
                trans = t_ref[r * splats + s, vs[v]]
                shade = ks[0] * gs[0][v] + ks[1] * gs[1][v] + ks[2] * gs[2][v]
                diff = shade - behind[v]
                behind[v] = behind[v] + alpha * diff
                weight = trans * alpha
                h = weight * diff
                w = (ypos[v] - m_y) * inv_y
                hw = h * w
                parts = [h, hw, hw * w] + [weight * gs[k][v] for k in range(3)]
                acc = parts if acc is None else [x + y for x, y in zip(acc, parts)]
            hu = acc[0] * u
            sums = [acc[0], hu, acc[1], hu * u, acc[1] * u, acc[2], acc[3], acc[4], acc[5]]
            for p in range(9):
                mbuf[pl.ds((p * splats + s) * 8, 8), :] = sums[p]
        blocks = []
        for p in range(9):
            total = mbuf[pl.ds(p * 64, 8, stride=8), :]
            for j in range(1, 8):
                total = total + mbuf[pl.ds(p * 64 + j, 8, stride=8), :]
            blocks.append(total)
        summed = jnp.dot(
            jnp.concatenate(blocks, 0), gather_out, precision=HI, preferred_element_type=jnp.float32
        )
        mask = x_ref[9, pl.ds(r, 1), :] == rank_row
        for p in range(9):
            red_ref[p, pl.ds(r, 1), :] = jnp.sum(
                jnp.where(mask, summed[p * splats:(p + 1) * splats], 0.0), 0, keepdims=True
            )
        return carry

    lax.fori_loop(0, regions, backward, 0)

    h0, hu, hv, huu, huv, hvv = [red_ref[p] for p in range(6)]
    squash = jnp.tanh(x_ref[4])
    rho = 0.9 * squash
    inv = 1.0 / (1.0 - rho * rho)
    grad_ref[0] = d_ref[2] * inv * (hu - rho * hv)
    grad_ref[1] = d_ref[3] * inv * (hv - rho * hu)
    grad_ref[2] = inv * (huu - rho * huv)
    grad_ref[3] = inv * (hvv - rho * huv)
    hq = inv * (huu - 2.0 * rho * huv + hvv)
    grad_ref[4] = inv * (huv - rho * hq) * (0.9 * (1.0 - squash * squash))
    grad_ref[5] = h0 * jax.nn.sigmoid(-x_ref[5])
    for k in range(3):
        tone = d_ref[7 + k]
        grad_ref[6 + k] = red_ref[6 + k] * tone * (1.0 - tone)


def render(received, flip_rows, wanted, spread):
    regions, group = received.shape[1:]
    rows = wanted.shape[1]
    nodes = 2 * regions - 1
    f32 = jnp.float32
    return pl.pallas_call(
        render_kernel,
        out_shape=(
            jax.ShapeDtypeStruct((rows, LANES), f32),
            jax.ShapeDtypeStruct((9, regions, group), f32),
        ),
        in_specs=[pl.BlockSpec(memory_space=pltpu.VMEM)] * 4,
        out_specs=(pl.BlockSpec(memory_space=pltpu.VMEM),) * 2,
        scratch_shapes=[
            pltpu.VMEM((NPAR, regions, group), f32),
            pltpu.VMEM((regions, NPAR * 8, LANES), f32),
            pltpu.VMEM((regions * 8, rows, LANES), f32),
            pltpu.VMEM((regions * 8, rows, LANES), f32),
            pltpu.VMEM((nodes, 4, rows, LANES), f32),
            pltpu.VMEM((nodes, 4, rows, LANES), f32),
            pltpu.VMEM((9 * 64, LANES), f32),
            pltpu.VMEM((9, regions, group), f32),
        ],
        compiler_params=pltpu.CompilerParams(vmem_limit_bytes=48 * 1024 * 1024),
    )(received, flip_rows, wanted, spread)


def uncertainty(stripe_feats, w_first, b_first, w_second):
    hidden = jax.nn.gelu(
        jnp.dot(stripe_feats, w_first, preferred_element_type=jnp.float32) + b_first
    ).astype(jnp.bfloat16)
    return 0.5 + jax.nn.softplus(jnp.dot(hidden, w_second, preferred_element_type=jnp.float32))


def shards(gaussians, depth, coverage, flips, features, w_first, b_first, w_second, target):
    regions = lax.axis_size("region")
    my_index = lax.axis_index("region")
    tile_count = depth.shape[1]
    splats = depth.shape[2]
    stripe_tiles = tile_count // regions
    group = stripe_tiles * splats
    span = LANES // stripe_tiles
    rows = TSIDE * TSIDE // span

    payload = jnp.concatenate(
        [
            gaussians[0],
            depth.reshape(1, tile_count * splats).astype(jnp.float32),
            jnp.repeat(coverage, splats, axis=1).astype(jnp.float32),
        ],
        0,
    ).reshape(11, regions, group)
    received = lax.all_to_all(payload, "region", 1, 1)
    spread = uncertainty(features, w_first, b_first, w_second)

    def to_rows(x):
        lead = x.shape[:-1]
        x = x.reshape(lead + (stripe_tiles, rows, span))
        return jnp.swapaxes(x, -3, -2).reshape(lead + (rows, LANES))

    my_flips = lax.dynamic_slice_in_dim(flips, my_index * stripe_tiles, stripe_tiles, 0)
    flip_rows = jnp.repeat(my_flips.T.astype(jnp.float32), span, axis=1)[:, None, :]
    loss, grads = render(received, flip_rows, to_rows(target), to_rows(spread))
    pixel_loss = jnp.swapaxes(loss.reshape(rows, stripe_tiles, span), 0, 1).reshape(-1)
    returned = lax.all_to_all(grads, "region", 1, 1)
    return (pixel_loss, returned.reshape(1, 9, tile_count * splats))


def solution(mesh):
    placed = (
        P("region", None, None),
        P("region", None, None),
        P("region", None),
        P(),
        P("region", None),
        P(),
        P(),
        P(),
        P(None, "region"),
    )
    return jax.shard_map(
        shards,
        mesh=mesh,
        in_specs=placed,
        out_specs=(P("region"), P("region", None, None)),
        check_vma=False,
    )
```

```python
import jax
import jax.numpy as jnp
from jax import lax
from jax.experimental import pallas as pl
from jax.experimental.pallas import tpu as pltpu
from jax.sharding import PartitionSpec as P

TSIDE = 16
LANES = 128
NPAR = 10
LOG2E = 1.4426950408889634
HI = lax.Precision.HIGHEST


def dot(x, y, transposed=False):
    dims = (((1,), (1 if transposed else 0,)), ((), ()))
    return lax.dot_general(x, y, dims, precision=HI, preferred_element_type=jnp.float32)


def same(shape, first, second):
    left = first(lax.broadcasted_iota(jnp.int32, shape, 0))
    right = second(lax.broadcasted_iota(jnp.int32, shape, 1))
    return (left == right).astype(jnp.float32)


def splat_kernel(
    gauss_ref, depth_ref, cover_ref, flips_ref, feat_hbm, first_ref, bias_ref, second_ref,
    target_ref, loss_ref, out_ref,
    feat_ref, feat_sem, send_ref, recv_ref, send_sem, recv_sem, gsend_ref, grecv_ref, gsend_sem,
    grecv_sem, x_ref, flip_ref, spread_ref, wanted_ref,
    d_ref, ex_ref, a_ref, t_ref, tree_ref, gtree_ref, mbuf, red_ref,
):
    regions, group = x_ref.shape[1:]
    splats = 8
    rows = wanted_ref.shape[1]
    nv = rows // 8
    stripe_tiles = group // splats
    span = LANES // stripe_tiles
    inner = regions - 1
    tile_count = depth_ref.shape[0]
    pixels = TSIDE * TSIDE
    me = lax.axis_index("region")

    load = pltpu.make_async_copy(feat_hbm, feat_ref, feat_sem)
    load.start()
    barrier = pltpu.get_barrier_semaphore()

    def greet(i, carry):
        pl.semaphore_signal(
            barrier, inc=1, device_id=(lax.rem(me + i, regions),),
            device_id_type=pl.DeviceIdType.MESH,
        )
        return carry

    lax.fori_loop(1, regions, greet, 0)

    owner = same((regions, tile_count), lambda i: i, lambda j: j // stripe_tiles)
    pick = same((splats, group), lambda i: i, lambda j: j & (splats - 1))
    place = same(
        (tile_count, group), lambda i: i & (stripe_tiles - 1), lambda j: j // splats
    )
    rank_rows = dot(owner, dot(depth_ref[...].astype(jnp.float32), pick) * place)
    cover_rows = dot(owner * cover_ref[...].astype(jnp.float32), place)
    for d in range(regions):
        send_ref[d, 0:9, :] = gauss_ref[:, d * group:(d + 1) * group]
        send_ref[d, 9:10, :] = rank_rows[d:d + 1]
        send_ref[d, 10:11, :] = cover_rows[d:d + 1]
    load.wait()

    block = max(16, span)
    per_block = block // span

    def network(j, carry):
        feats = feat_ref[:, pl.ds(pl.multiple_of(j * block, block), block), :]
        feats = feats.reshape(stripe_tiles * block, feat_ref.shape[2])
        hidden = jax.nn.gelu(
            jnp.dot(feats, first_ref[...], preferred_element_type=jnp.float32) + bias_ref[...]
        )
        hidden = hidden.reshape(stripe_tiles, per_block, span, hidden.shape[-1])
        for i in range(per_block):
            part = hidden[:, i].reshape(LANES, hidden.shape[-1]).astype(jnp.bfloat16)
            logits = lax.dot_general(
                second_ref[...], part, (((1,), (1,)), ((), ())),
                preferred_element_type=jnp.float32,
            )
            spread_ref[pl.ds(j * per_block + i, 1), :] = logits[0:1]
        return carry

    steps = pixels // block
    lax.fori_loop(0, steps // 2, network, 0)
    pl.semaphore_wait(barrier, regions - 1)

    def exchange(i, src, dst, ssem, rsem):
        peer = lax.rem(me + i, regions)
        return pltpu.make_async_remote_copy(
            src_ref=src.at[peer], dst_ref=dst.at[me], send_sem=ssem.at[peer],
            recv_sem=rsem.at[me], device_id=(peer,), device_id_type=pl.DeviceIdType.MESH,
        )

    def arrival(i, src, dst, ssem, rsem):
        peer = lax.rem(me + i, regions)
        return pltpu.make_async_remote_copy(
            src_ref=src.at[peer], dst_ref=dst.at[peer], send_sem=ssem.at[peer],
            recv_sem=rsem.at[peer], device_id=(peer,), device_id_type=pl.DeviceIdType.MESH,
        )

    there = (send_ref, recv_ref, send_sem, recv_sem)
    back_way = (gsend_ref, grecv_ref, gsend_sem, grecv_sem)

    def send(i, carry):
        exchange(i, *there).start()
        return carry

    lax.fori_loop(1, regions, send, 0)
    recv_ref[me] = send_ref[me]
    lax.fori_loop(steps // 2, steps, network, 0)

    tile_lane = same((LANES, stripe_tiles), lambda i: i // span, lambda j: j)
    lane_pixel = same((LANES, pixels), lambda i: i & (span - 1), lambda j: j & (span - 1))
    row_pixel = same((rows, pixels), lambda i: i, lambda j: j // span)
    for k in range(3):
        flat = jnp.concatenate(
            [target_ref[k:k + 1, t * pixels:(t + 1) * pixels] for t in range(stripe_tiles)], 0
        )
        wanted_ref[k] = dot(row_pixel, dot(tile_lane, flat) * lane_pixel, True)
    lane_tile = same((stripe_tiles, LANES), lambda i: i, lambda j: j // span)
    flip_ref[...] = dot(flips_ref[...], lane_tile)

    def arrive(i, carry):
        arrival(i, *there).wait()
        return carry

    lax.fori_loop(1, regions, arrive, 0)
    for p in range(11):
        x_ref[p] = recv_ref[:, p, :]

    sub = lax.broadcasted_iota(jnp.int32, (8, LANES), 0)
    lane = lax.broadcasted_iota(jnp.int32, (8, LANES), 1)
    pix = sub * span + (lane & (span - 1))
    xpos = (pix & (TSIDE - 1)).astype(jnp.float32) + 0.5
    ypos = [((pix + 8 * v * span) // TSIDE).astype(jnp.float32) + 0.5 for v in range(nv)]
    vs = [slice(8 * v, 8 * v + 8) for v in range(nv)]

    spread_in = (
        lax.broadcasted_iota(jnp.int32, (group, LANES), 0) // splats
        == lax.broadcasted_iota(jnp.int32, (group, LANES), 1) // span
    ).astype(jnp.float32)
    gather_out = (
        lax.broadcasted_iota(jnp.int32, (LANES, group), 0) // span
        == lax.broadcasted_iota(jnp.int32, (LANES, group), 1) // splats
    ).astype(jnp.float32)
    rank_row = lax.broadcasted_iota(jnp.int32, (splats, group), 0).astype(jnp.float32)

    rho = 0.9 * jnp.tanh(x_ref[4])
    norm = lax.rsqrt(1.0 - rho * rho)
    d_ref[0] = x_ref[0]
    d_ref[1] = x_ref[1]
    d_ref[2] = jnp.exp(-x_ref[2])
    d_ref[3] = jnp.exp(-x_ref[3])
    d_ref[4] = norm
    d_ref[5] = rho * norm
    d_ref[6] = 0.99 * jax.nn.sigmoid(x_ref[5]) * x_ref[10]
    for k in range(3):
        d_ref[7 + k] = jax.nn.sigmoid(x_ref[6 + k])

    def expand(r, carry):
        mask = x_ref[9, pl.ds(r, 1), :] == rank_row
        picked = [
            jnp.where(mask, jnp.broadcast_to(d_ref[p, pl.ds(r, 1), :], (splats, group)), 0.0)
            for p in range(NPAR)
        ]
        ex_ref[r] = jnp.dot(
            jnp.concatenate(picked, 0), spread_in, precision=HI, preferred_element_type=jnp.float32
        )
        return carry

    lax.fori_loop(0, regions, expand, 0, unroll=2)

    def row(r, p, s):
        return ex_ref[r, pl.ds(p * splats + s, 1), :]

    def forward(r, carry):
        trans = [jnp.ones((8, LANES), jnp.float32)] * nv
        color = [[jnp.zeros((8, LANES), jnp.float32)] * nv for _ in range(3)]
        for s in range(splats):
            u = (xpos - row(r, 0, s)) * row(r, 2, s)
            us = u * row(r, 4, s)
            m_y, inv_y, skew, op = row(r, 1, s), row(r, 3, s), row(r, 5, s), row(r, 6, s)
            ks = [row(r, 7 + k, s) for k in range(3)]
            for v in range(nv):
                w = (ypos[v] - m_y) * inv_y
                p = us - skew * w
                alpha = op * jnp.exp2((p * p + w * w) * (-0.5 * LOG2E))
                a_ref[r * splats + s, vs[v]] = alpha
                t_ref[r * splats + s, vs[v]] = trans[v]
                weight = trans[v] * alpha
                for k in range(3):
                    color[k][v] = color[k][v] + weight * ks[k]
                trans[v] = trans[v] * (1.0 - alpha)
        for v in range(nv):
            for k in range(3):
                tree_ref[inner + r, k, vs[v]] = color[k][v]
            tree_ref[inner + r, 3, vs[v]] = trans[v]
        return carry

    lax.fori_loop(0, regions, forward, 0)

    def merge(i, carry):
        n = inner - 1 - i
        flip = jnp.broadcast_to(flip_ref[pl.ds(n, 1), :], (8, LANES)) > 0.0
        for v in range(nv):
            low = [tree_ref[2 * n + 1, k, vs[v]] for k in range(4)]
            high = [tree_ref[2 * n + 2, k, vs[v]] for k in range(4)]
            front = [jnp.where(flip, h, l) for l, h in zip(low, high)]
            back = [jnp.where(flip, l, h) for l, h in zip(low, high)]
            for k in range(3):
                tree_ref[n, k, vs[v]] = front[k] + front[3] * back[k]
            tree_ref[n, 3, vs[v]] = front[3] * back[3]
        return carry

    lax.fori_loop(0, inner, merge, 0)

    losses = []
    for v in range(nv):
        logit = spread_ref[vs[v]]
        spread = 0.5 + jnp.maximum(logit, 0.0) + jnp.log1p(jnp.exp(-jnp.abs(logit)))
        inv_square = 1.0 / (spread * spread)
        clear = tree_ref[0, 3, vs[v]]
        residual = [tree_ref[0, k, vs[v]] + clear - wanted_ref[k, vs[v]] for k in range(3)]
        total = residual[0] * residual[0] + residual[1] * residual[1] + residual[2] * residual[2]
        losses.append(0.5 * total * inv_square + jnp.log(spread))
        gs = [res * inv_square for res in residual]
        for k in range(3):
            gtree_ref[0, k, vs[v]] = gs[k]
        gtree_ref[0, 3, vs[v]] = gs[0] + gs[1] + gs[2]

    pixel_row = same((pixels, rows), lambda i: i // span, lambda j: j)
    pixel_lane = same((pixels, LANES), lambda i: i & (span - 1), lambda j: j & (span - 1))
    flat = dot(lane_tile, dot(pixel_row, jnp.concatenate(losses, 0)) * pixel_lane, True)
    for t in range(stripe_tiles):
        loss_ref[0:1, t * pixels:(t + 1) * pixels] = flat[t:t + 1]

    def split(n, carry):
        flip = jnp.broadcast_to(flip_ref[pl.ds(n, 1), :], (8, LANES)) > 0.0
        for v in range(nv):
            low = [tree_ref[2 * n + 1, k, vs[v]] for k in range(4)]
            high = [tree_ref[2 * n + 2, k, vs[v]] for k in range(4)]
            g = [gtree_ref[n, k, vs[v]] for k in range(4)]
            front_t = jnp.where(flip, high[3], low[3])
            back = [jnp.where(flip, l, h) for l, h in zip(low, high)]
            g_front_t = g[0] * back[0] + g[1] * back[1] + g[2] * back[2] + g[3] * back[3]
            for k in range(4):
                g_front = g[k] if k < 3 else g_front_t
                g_back = front_t * g[k]
                gtree_ref[2 * n + 1, k, vs[v]] = jnp.where(flip, g_back, g_front)
                gtree_ref[2 * n + 2, k, vs[v]] = jnp.where(flip, g_front, g_back)
        return carry

    lax.fori_loop(0, inner, split, 0)

    def backward(r, carry):
        gs = [[gtree_ref[inner + r, k, vs[v]] for v in range(nv)] for k in range(3)]
        behind = [gtree_ref[inner + r, 3, vs[v]] for v in range(nv)]
        for s in reversed(range(splats)):
            u = (xpos - row(r, 0, s)) * row(r, 2, s)
            m_y, inv_y = row(r, 1, s), row(r, 3, s)
            ks = [row(r, 7 + k, s) for k in range(3)]
            acc = None
            for v in range(nv):
                alpha = a_ref[r * splats + s, vs[v]]
                trans = t_ref[r * splats + s, vs[v]]
                shade = ks[0] * gs[0][v] + ks[1] * gs[1][v] + ks[2] * gs[2][v]
                diff = shade - behind[v]
                behind[v] = behind[v] + alpha * diff
                weight = trans * alpha
                h = weight * diff
                w = (ypos[v] - m_y) * inv_y
                hw = h * w
                parts = [h, hw, hw * w] + [weight * gs[k][v] for k in range(3)]
                acc = parts if acc is None else [x + y for x, y in zip(acc, parts)]
            hu = acc[0] * u
            sums = [acc[0], hu, acc[1], hu * u, acc[1] * u, acc[2], acc[3], acc[4], acc[5]]
            for p in range(9):
                mbuf[pl.ds((p * splats + s) * 8, 8), :] = sums[p]
        blocks = []
        for p in range(9):
            total = mbuf[pl.ds(p * 64, 8, stride=8), :]
            for j in range(1, 8):
                total = total + mbuf[pl.ds(p * 64 + j, 8, stride=8), :]
            blocks.append(total)
        summed = jnp.dot(
            jnp.concatenate(blocks, 0), gather_out, precision=HI, preferred_element_type=jnp.float32
        )
        mask = x_ref[9, pl.ds(r, 1), :] == rank_row
        for p in range(9):
            red_ref[p, pl.ds(r, 1), :] = jnp.sum(
                jnp.where(mask, summed[p * splats:(p + 1) * splats], 0.0), 0, keepdims=True
            )
        return carry

    batch = 8
    batches = regions // batch

    def finish(i, carry):
        which = lax.rem(i + 1 + me // batch, batches)
        base = pl.multiple_of(which * batch, batch)
        lax.fori_loop(base, base + batch, backward, 0)
        some = pl.ds(base, batch)
        h0, hu, hv, huu, huv, hvv = [red_ref[p, some, :] for p in range(6)]
        squash = jnp.tanh(x_ref[4, some, :])
        rho = 0.9 * squash
        inv = 1.0 / (1.0 - rho * rho)
        hq = inv * (huu - 2.0 * rho * huv + hvv)
        results = [
            d_ref[2, some, :] * inv * (hu - rho * hv),
            d_ref[3, some, :] * inv * (hv - rho * hu),
            inv * (huu - rho * huv),
            inv * (hvv - rho * huv),
            inv * (huv - rho * hq) * (0.9 * (1.0 - squash * squash)),
            h0 * jax.nn.sigmoid(-x_ref[5, some, :]),
        ]
        for k in range(3):
            tone = d_ref[7 + k, some, :]
            results.append(red_ref[6 + k, some, :] * tone * (1.0 - tone))
        for j in range(batch):
            gsend_ref[base + j, 0:9, :] = jnp.concatenate([x[j:j + 1] for x in results], 0)
        for j in range(batch):
            peer = base + j

            @pl.when(peer != me)
            def _():
                pltpu.make_async_remote_copy(
                    src_ref=gsend_ref.at[peer], dst_ref=grecv_ref.at[me],
                    send_sem=gsend_sem.at[peer], recv_sem=grecv_sem.at[me],
                    device_id=(peer,), device_id_type=pl.DeviceIdType.MESH,
                ).start()

        return carry

    lax.fori_loop(0, batches, finish, 0)
    grecv_ref[me] = gsend_ref[me]

    def collect(i, carry):
        arrival(i, *back_way).wait()
        return carry

    lax.fori_loop(1, regions, collect, 0)
    for d in range(regions):
        out_ref[:, d * group:(d + 1) * group] = grecv_ref[d, 0:9, :]


def shards(gaussians, depth, coverage, flips, features, w_first, b_first, w_second, target):
    regions = lax.axis_size("region")
    my_index = lax.axis_index("region")
    tile_count = depth.shape[1]
    splats = depth.shape[2]
    stripe_tiles = tile_count // regions
    group = stripe_tiles * splats
    pixels = TSIDE * TSIDE
    rows = pixels * stripe_tiles // LANES
    nodes = 2 * regions - 1
    width = features.shape[1]
    f32 = jnp.float32
    my_flips = lax.dynamic_slice_in_dim(flips, my_index * stripe_tiles, stripe_tiles, 0)
    vmem = pl.BlockSpec(memory_space=pltpu.VMEM)
    dma = pltpu.SemaphoreType.DMA
    loss, grads = pl.pallas_call(
        splat_kernel,
        out_shape=(
            jax.ShapeDtypeStruct((1, stripe_tiles * pixels), f32),
            jax.ShapeDtypeStruct((9, tile_count * splats), f32),
        ),
        in_specs=[vmem] * 4 + [pl.BlockSpec(memory_space=pl.ANY)] + [vmem] * 4,
        out_specs=(vmem, vmem),
        scratch_shapes=[
            pltpu.VMEM((stripe_tiles, pixels, width), features.dtype),
            dma(()),
            pltpu.VMEM((regions, 16, group), f32),
            pltpu.VMEM((regions, 16, group), f32),
            dma((regions,)),
            dma((regions,)),
            pltpu.VMEM((regions, 16, group), f32),
            pltpu.VMEM((regions, 16, group), f32),
            dma((regions,)),
            dma((regions,)),
            pltpu.VMEM((11, regions, group), f32),
            pltpu.VMEM((regions - 1, LANES), f32),
            pltpu.VMEM((rows, LANES), f32),
            pltpu.VMEM((3, rows, LANES), f32),
            pltpu.VMEM((NPAR, regions, group), f32),
            pltpu.VMEM((regions, NPAR * 8, LANES), f32),
            pltpu.VMEM((regions * 8, rows, LANES), f32),
            pltpu.VMEM((regions * 8, rows, LANES), f32),
            pltpu.VMEM((nodes, 4, rows, LANES), f32),
            pltpu.VMEM((nodes, 4, rows, LANES), f32),
            pltpu.VMEM((9 * 64, LANES), f32),
            pltpu.VMEM((9, regions, group), f32),
        ],
        compiler_params=pltpu.CompilerParams(
            vmem_limit_bytes=56 * 1024 * 1024, collective_id=0, has_side_effects=True
        ),
    )(
        gaussians[0],
        depth[0],
        coverage,
        my_flips.T.astype(f32),
        features.reshape(stripe_tiles, pixels, width),
        w_first,
        b_first[None],
        jnp.broadcast_to(w_second[None], (16, width)),
        target,
    )
    return (loss.reshape(-1), grads[None])


def solution(mesh):
    placed = (
        P("region", None, None),
        P("region", None, None),
        P("region", None),
        P(),
        P("region", None),
        P(),
        P(),
        P(),
        P(None, "region"),
    )
    return jax.shard_map(
        shards,
        mesh=mesh,
        in_specs=placed,
        out_specs=(P("region"), P("region", None, None)),
        check_vma=False,
    )
```

```python
import jax
import jax.numpy as jnp
from jax import lax
from jax.experimental import pallas as pl
from jax.experimental.pallas import tpu as pltpu
from jax.sharding import PartitionSpec as P

TSIDE = 16
LANES = 128
NPAR = 10
LOG2E = 1.4426950408889634
HI = lax.Precision.HIGHEST


def dot(x, y, transposed=False, selector=1):
    dims = (((1,), (1 if transposed else 0,)), ((), ()))
    bf16 = jnp.bfloat16
    sel, val = (y, x) if selector == 1 else (x, y)
    sel = sel.astype(bf16)
    total = None
    for _ in range(3):
        piece = val.astype(bf16)
        val = val - piece.astype(jnp.float32)
        pair = (piece, sel) if selector == 1 else (sel, piece)
        part = lax.dot_general(*pair, dims, preferred_element_type=jnp.float32)
        total = part if total is None else total + part
    return total


def same(shape, first, second):
    left = first(lax.broadcasted_iota(jnp.int32, shape, 0))
    right = second(lax.broadcasted_iota(jnp.int32, shape, 1))
    return (left == right).astype(jnp.float32)


def splat_kernel(
    gauss_ref, depth_ref, cover_ref, flips_ref, feat_hbm, first_ref, bias_ref, second_ref,
    target_ref, loss_ref, out_ref,
    feat_ref, feat_sem, send_ref, recv_ref, send_sem, recv_sem, gsend_ref, grecv_ref, gsend_sem,
    grecv_sem, x_ref, flip_ref, spread_ref, wanted_ref,
    d_ref, ex_ref, a_ref, t_ref, tree_ref, gtree_ref, mbuf, sum_ref, red_ref,
):
    regions, group = x_ref.shape[1:]
    splats = 8
    rows = wanted_ref.shape[1]
    nv = rows // 8
    stripe_tiles = group // splats
    span = LANES // stripe_tiles
    inner = regions - 1
    tile_count = depth_ref.shape[1]
    pixels = TSIDE * TSIDE
    me = lax.axis_index("region")

    load = pltpu.make_async_copy(feat_hbm, feat_ref, feat_sem)
    load.start()
    barrier = pltpu.get_barrier_semaphore()

    def greet(i, carry):
        pl.semaphore_signal(
            barrier, inc=1, device_id=(lax.rem(me + i, regions),),
            device_id_type=pl.DeviceIdType.MESH,
        )
        return carry

    lax.fori_loop(1, regions, greet, 0)

    owner = same((regions, tile_count), lambda i: i, lambda j: j // stripe_tiles)
    place = same(
        (tile_count, group), lambda i: i & (stripe_tiles - 1), lambda j: j // splats
    )
    marks = [owner * depth_ref[g:g + 1, :].astype(jnp.float32) for g in range(splats)]
    marks.append(owner * cover_ref[...].astype(jnp.float32))
    marked = jnp.dot(
        jnp.concatenate(marks, 0).astype(jnp.bfloat16), place.astype(jnp.bfloat16),
        preferred_element_type=jnp.float32,
    )
    which_splat = lax.broadcasted_iota(jnp.int32, (regions, group), 1) & (splats - 1)
    rank_rows = jnp.zeros((regions, group), jnp.float32)
    for g in range(splats):
        rank_rows = jnp.where(which_splat == g, marked[g * regions:(g + 1) * regions], rank_rows)
    cover_rows = marked[splats * regions:]
    for d in range(regions):
        for p in range(9):
            send_ref[d, p:p + 1, :] = gauss_ref[p, :, d * group:(d + 1) * group]
        send_ref[d, 9:10, :] = rank_rows[d:d + 1]
        send_ref[d, 10:11, :] = cover_rows[d:d + 1]
    bias = bias_ref[...].reshape(1, bias_ref.shape[0])
    second = jnp.broadcast_to(
        second_ref[...].astype(jnp.float32).reshape(1, second_ref.shape[0]),
        (16, second_ref.shape[0]),
    ).astype(jnp.bfloat16)
    load.wait()

    block = max(16, span)
    per_block = block // span

    def network(j, carry):
        feats = feat_ref[:, pl.ds(pl.multiple_of(j * block, block), block), :]
        feats = feats.reshape(stripe_tiles * block, feat_ref.shape[2])
        hidden = jax.nn.gelu(
            jnp.dot(feats, first_ref[...], preferred_element_type=jnp.float32) + bias
        )
        hidden = hidden.reshape(stripe_tiles, per_block, span, hidden.shape[-1])
        for i in range(per_block):
            part = hidden[:, i].reshape(LANES, hidden.shape[-1]).astype(jnp.bfloat16)
            logits = lax.dot_general(
                second, part, (((1,), (1,)), ((), ())),
                preferred_element_type=jnp.float32,
            )
            spread_ref[pl.ds(j * per_block + i, 1), :] = logits[0:1]
        return carry

    steps = pixels // block
    lax.fori_loop(0, steps // 2, network, 0, unroll=2)
    pl.semaphore_wait(barrier, regions - 1)

    def exchange(i, src, dst, ssem, rsem):
        peer = lax.rem(me + i, regions)
        return pltpu.make_async_remote_copy(
            src_ref=src.at[peer], dst_ref=dst.at[me], send_sem=ssem.at[peer],
            recv_sem=rsem.at[me], device_id=(peer,), device_id_type=pl.DeviceIdType.MESH,
        )

    def arrival(i, src, dst, ssem, rsem):
        peer = lax.rem(me + i, regions)
        return pltpu.make_async_remote_copy(
            src_ref=src.at[peer], dst_ref=dst.at[peer], send_sem=ssem.at[peer],
            recv_sem=rsem.at[peer], device_id=(peer,), device_id_type=pl.DeviceIdType.MESH,
        )

    there = (send_ref, recv_ref, send_sem, recv_sem)
    back_way = (gsend_ref, grecv_ref, gsend_sem, grecv_sem)

    def send(i, carry):
        exchange(i, *there).start()
        return carry

    lax.fori_loop(1, regions, send, 0)
    recv_ref[me] = send_ref[me]
    lax.fori_loop(steps // 2, steps, network, 0, unroll=2)

    tile_lane = same((LANES, stripe_tiles), lambda i: i // span, lambda j: j)
    lane_pixel = same((LANES, pixels), lambda i: i & (span - 1), lambda j: j & (span - 1))
    row_pixel = same((rows, pixels), lambda i: i, lambda j: j // span)
    for k in range(3):
        flat = jnp.concatenate(
            [target_ref[k:k + 1, t * pixels:(t + 1) * pixels] for t in range(stripe_tiles)], 0
        )
        wanted_ref[k] = dot(row_pixel, dot(tile_lane, flat, selector=0) * lane_pixel, True, selector=0)
    lane_tile = same((stripe_tiles, LANES), lambda i: i, lambda j: j // span)
    my_tiles = same(
        (tile_count, LANES), lambda i: i - me * stripe_tiles, lambda j: j // span
    ).astype(jnp.bfloat16)
    flip_ref[...] = jnp.dot(
        flips_ref[...].astype(jnp.float32).astype(jnp.bfloat16), my_tiles,
        preferred_element_type=jnp.float32,
    )

    def arrive(i, carry):
        arrival(i, *there).wait()
        return carry

    lax.fori_loop(1, regions, arrive, 0)
    for p in range(11):
        x_ref[p] = recv_ref[:, p, :]

    sub = lax.broadcasted_iota(jnp.int32, (8, LANES), 0)
    lane = lax.broadcasted_iota(jnp.int32, (8, LANES), 1)
    pix = sub * span + (lane & (span - 1))
    xpos = (pix & (TSIDE - 1)).astype(jnp.float32) + 0.5
    ypos = [((pix + 8 * v * span) // TSIDE).astype(jnp.float32) + 0.5 for v in range(nv)]
    vs = [slice(8 * v, 8 * v + 8) for v in range(nv)]

    spread_in = (
        lax.broadcasted_iota(jnp.int32, (group, LANES), 0) // splats
        == lax.broadcasted_iota(jnp.int32, (group, LANES), 1) // span
    ).astype(jnp.float32)
    gather_out = (
        lax.broadcasted_iota(jnp.int32, (LANES, group), 0) // span
        == lax.broadcasted_iota(jnp.int32, (LANES, group), 1) // splats
    ).astype(jnp.float32)
    rank_row = lax.broadcasted_iota(jnp.int32, (splats, group), 0).astype(jnp.float32)

    rho = 0.9 * jnp.tanh(x_ref[4])
    norm = lax.rsqrt(1.0 - rho * rho)
    d_ref[0] = x_ref[0]
    d_ref[1] = x_ref[1]
    d_ref[2] = jnp.exp(-x_ref[2])
    d_ref[3] = jnp.exp(-x_ref[3])
    d_ref[4] = norm
    d_ref[5] = rho * norm
    d_ref[6] = 0.99 * jax.nn.sigmoid(x_ref[5]) * x_ref[10]
    for k in range(3):
        d_ref[7 + k] = jax.nn.sigmoid(x_ref[6 + k])

    def expand(r, carry):
        mask = x_ref[9, pl.ds(r, 1), :] == rank_row
        picked = [
            jnp.where(mask, jnp.broadcast_to(d_ref[p, pl.ds(r, 1), :], (splats, group)), 0.0)
            for p in range(NPAR)
        ]
        ex_ref[r] = dot(jnp.concatenate(picked, 0), spread_in)
        return carry

    lax.fori_loop(0, regions, expand, 0, unroll=4)

    def row(r, p, s):
        return ex_ref[r, pl.ds(p * splats + s, 1), :]

    def forward(r, carry):
        trans = [jnp.ones((8, LANES), jnp.float32)] * nv
        color = [[jnp.zeros((8, LANES), jnp.float32)] * nv for _ in range(3)]
        for s in range(splats):
            u = (xpos - row(r, 0, s)) * row(r, 2, s)
            us = u * row(r, 4, s)
            m_y, inv_y, skew, op = row(r, 1, s), row(r, 3, s), row(r, 5, s), row(r, 6, s)
            ks = [row(r, 7 + k, s) for k in range(3)]
            for v in range(nv):
                w = (ypos[v] - m_y) * inv_y
                p = us - skew * w
                alpha = op * jnp.exp2((p * p + w * w) * (-0.5 * LOG2E))
                a_ref[r * splats + s, vs[v]] = alpha
                t_ref[r * splats + s, vs[v]] = trans[v]
                weight = trans[v] * alpha
                for k in range(3):
                    color[k][v] = color[k][v] + weight * ks[k]
                trans[v] = trans[v] * (1.0 - alpha)
        for v in range(nv):
            for k in range(3):
                tree_ref[inner + r, k, vs[v]] = color[k][v]
            tree_ref[inner + r, 3, vs[v]] = trans[v]
        return carry

    lax.fori_loop(0, regions, forward, 0)

    def merge(i, carry):
        n = inner - 1 - i
        flip = jnp.broadcast_to(flip_ref[pl.ds(n, 1), :], (8, LANES)) > 0.0
        for v in range(nv):
            low = [tree_ref[2 * n + 1, k, vs[v]] for k in range(4)]
            high = [tree_ref[2 * n + 2, k, vs[v]] for k in range(4)]
            front = [jnp.where(flip, h, l) for l, h in zip(low, high)]
            back = [jnp.where(flip, l, h) for l, h in zip(low, high)]
            for k in range(3):
                tree_ref[n, k, vs[v]] = front[k] + front[3] * back[k]
            tree_ref[n, 3, vs[v]] = front[3] * back[3]
        return carry

    lax.fori_loop(0, inner, merge, 0)

    losses = []
    for v in range(nv):
        logit = spread_ref[vs[v]]
        spread = 0.5 + jnp.maximum(logit, 0.0) + jnp.log1p(jnp.exp(-jnp.abs(logit)))
        inv_square = 1.0 / (spread * spread)
        clear = tree_ref[0, 3, vs[v]]
        residual = [tree_ref[0, k, vs[v]] + clear - wanted_ref[k, vs[v]] for k in range(3)]
        total = residual[0] * residual[0] + residual[1] * residual[1] + residual[2] * residual[2]
        losses.append(0.5 * total * inv_square + jnp.log(spread))
        gs = [res * inv_square for res in residual]
        for k in range(3):
            gtree_ref[0, k, vs[v]] = gs[k]
        gtree_ref[0, 3, vs[v]] = gs[0] + gs[1] + gs[2]

    pixel_row = same((pixels, rows), lambda i: i // span, lambda j: j)
    pixel_lane = same((pixels, LANES), lambda i: i & (span - 1), lambda j: j & (span - 1))
    flat = dot(lane_tile, dot(pixel_row, jnp.concatenate(losses, 0), selector=0) * pixel_lane, True, selector=0)
    for t in range(stripe_tiles):
        loss_ref[0:1, t * pixels:(t + 1) * pixels] = flat[t:t + 1]

    def split(n, carry):
        flip = jnp.broadcast_to(flip_ref[pl.ds(n, 1), :], (8, LANES)) > 0.0
        for v in range(nv):
            low = [tree_ref[2 * n + 1, k, vs[v]] for k in range(4)]
            high = [tree_ref[2 * n + 2, k, vs[v]] for k in range(4)]
            g = [gtree_ref[n, k, vs[v]] for k in range(4)]
            front_t = jnp.where(flip, high[3], low[3])
            back = [jnp.where(flip, l, h) for l, h in zip(low, high)]
            g_front_t = g[0] * back[0] + g[1] * back[1] + g[2] * back[2] + g[3] * back[3]
            for k in range(4):
                g_front = g[k] if k < 3 else g_front_t
                g_back = front_t * g[k]
                gtree_ref[2 * n + 1, k, vs[v]] = jnp.where(flip, g_back, g_front)
                gtree_ref[2 * n + 2, k, vs[v]] = jnp.where(flip, g_front, g_back)
        return carry

    lax.fori_loop(0, inner, split, 0)

    def backward(r, carry):
        gs = [[gtree_ref[inner + r, k, vs[v]] for v in range(nv)] for k in range(3)]
        behind = [gtree_ref[inner + r, 3, vs[v]] for v in range(nv)]
        for s in reversed(range(splats)):
            u = (xpos - row(r, 0, s)) * row(r, 2, s)
            m_y, inv_y = row(r, 1, s), row(r, 3, s)
            ks = [row(r, 7 + k, s) for k in range(3)]
            acc = None
            for v in range(nv):
                alpha = a_ref[r * splats + s, vs[v]]
                trans = t_ref[r * splats + s, vs[v]]
                shade = ks[0] * gs[0][v] + ks[1] * gs[1][v] + ks[2] * gs[2][v]
                diff = shade - behind[v]
                behind[v] = behind[v] + alpha * diff
                weight = trans * alpha
                h = weight * diff
                w = (ypos[v] - m_y) * inv_y
                hw = h * w
                parts = [h, hw, hw * w] + [weight * gs[k][v] for k in range(3)]
                acc = parts if acc is None else [x + y for x, y in zip(acc, parts)]
            hu = acc[0] * u
            sums = [acc[0], hu, acc[1], hu * u, acc[1] * u, acc[2], acc[3], acc[4], acc[5]]
            for p in range(9):
                mbuf[pl.ds((p * splats + s) * 8, 8), :] = sums[p]
        for p in range(9):
            total = mbuf[pl.ds(p * 64, 8, stride=8), :]
            for j in range(1, 8):
                total = total + mbuf[pl.ds(p * 64 + j, 8, stride=8), :]
            sum_ref[lax.rem(r, 8), p * splats:(p + 1) * splats, :] = total
        return carry

    batch = 8
    batches = regions // batch

    def finish(i, carry):
        which = lax.rem(i + 1 + me // batch, batches)
        base = pl.multiple_of(which * batch, batch)
        lax.fori_loop(base, base + batch, backward, 0)
        summed = dot(sum_ref[...].reshape(batch * 9 * splats, LANES), gather_out)
        for j in range(batch):
            mask = x_ref[9, pl.ds(base + j, 1), :] == rank_row
            for p in range(9):
                first = (j * 9 + p) * splats
                red_ref[p, pl.ds(base + j, 1), :] = jnp.sum(
                    jnp.where(mask, summed[first:first + splats], 0.0), 0, keepdims=True
                )
        some = pl.ds(base, batch)
        h0, hu, hv, huu, huv, hvv = [red_ref[p, some, :] for p in range(6)]
        squash = jnp.tanh(x_ref[4, some, :])
        rho = 0.9 * squash
        inv = 1.0 / (1.0 - rho * rho)
        hq = inv * (huu - 2.0 * rho * huv + hvv)
        results = [
            d_ref[2, some, :] * inv * (hu - rho * hv),
            d_ref[3, some, :] * inv * (hv - rho * hu),
            inv * (huu - rho * huv),
            inv * (hvv - rho * huv),
            inv * (huv - rho * hq) * (0.9 * (1.0 - squash * squash)),
            h0 * jax.nn.sigmoid(-x_ref[5, some, :]),
        ]
        for k in range(3):
            tone = d_ref[7 + k, some, :]
            results.append(red_ref[6 + k, some, :] * tone * (1.0 - tone))
        for j in range(batch):
            gsend_ref[base + j, 0:9, :] = jnp.concatenate([x[j:j + 1] for x in results], 0)
        for j in range(batch):
            peer = base + j

            @pl.when(peer != me)
            def _():
                pltpu.make_async_remote_copy(
                    src_ref=gsend_ref.at[peer], dst_ref=grecv_ref.at[me],
                    send_sem=gsend_sem.at[peer], recv_sem=grecv_sem.at[me],
                    device_id=(peer,), device_id_type=pl.DeviceIdType.MESH,
                ).start()

        return carry

    lax.fori_loop(0, batches, finish, 0)
    grecv_ref[me] = gsend_ref[me]

    def collect(i, carry):
        arrival(i, *back_way).wait()
        return carry

    lax.fori_loop(1, regions, collect, 0)
    for d in range(regions):
        for p in range(9):
            out_ref[p, :, d * group:(d + 1) * group] = grecv_ref[d, p:p + 1, :]


def hand_over(loss_in, grads_in, loss_out, grads_out):
    loss_out[...] = loss_in[...]
    grads_out[...] = grads_in[...]


def shards(gaussians, depth, coverage, flips, features, w_first, b_first, w_second, target):
    regions = lax.axis_size("region")
    tile_count = depth.shape[1]
    splats = depth.shape[2]
    stripe_tiles = tile_count // regions
    group = stripe_tiles * splats
    pixels = TSIDE * TSIDE
    rows = pixels * stripe_tiles // LANES
    nodes = 2 * regions - 1
    width = features.shape[1]
    f32 = jnp.float32
    vmem = pl.BlockSpec(memory_space=pltpu.VMEM)
    dma = pltpu.SemaphoreType.DMA
    loss, grads = pl.pallas_call(
        splat_kernel,
        out_shape=(
            jax.ShapeDtypeStruct((1, stripe_tiles * pixels), f32),
            jax.ShapeDtypeStruct((9, 1, tile_count * splats), f32),
        ),
        in_specs=[vmem] * 4 + [pl.BlockSpec(memory_space=pl.ANY)] + [vmem] * 4,
        out_specs=(vmem, vmem),
        scratch_shapes=[
            pltpu.VMEM((stripe_tiles, pixels, width), features.dtype),
            dma(()),
            pltpu.VMEM((regions, 16, group), f32),
            pltpu.VMEM((regions, 16, group), f32),
            dma((regions,)),
            dma((regions,)),
            pltpu.VMEM((regions, 16, group), f32),
            pltpu.VMEM((regions, 16, group), f32),
            dma((regions,)),
            dma((regions,)),
            pltpu.VMEM((11, regions, group), f32),
            pltpu.VMEM((regions - 1, LANES), f32),
            pltpu.VMEM((rows, LANES), f32),
            pltpu.VMEM((3, rows, LANES), f32),
            pltpu.VMEM((NPAR, regions, group), f32),
            pltpu.VMEM((regions, NPAR * 8, LANES), f32),
            pltpu.VMEM((regions * 8, rows, LANES), f32),
            pltpu.VMEM((regions * 8, rows, LANES), f32),
            pltpu.VMEM((nodes, 4, rows, LANES), f32),
            pltpu.VMEM((nodes, 4, rows, LANES), f32),
            pltpu.VMEM((9 * 64, LANES), f32),
            pltpu.VMEM((8, 9 * 8, LANES), f32),
            pltpu.VMEM((9, regions, group), f32),
        ],
        compiler_params=pltpu.CompilerParams(
            vmem_limit_bytes=56 * 1024 * 1024, collective_id=0, has_side_effects=True
        ),
    )(
        jnp.swapaxes(gaussians, 0, 1),
        depth[0].T,
        coverage,
        flips.T,
        features.reshape(stripe_tiles, pixels, width),
        w_first,
        b_first,
        w_second,
        target,
    )
    loss, grads = pl.pallas_call(
        hand_over,
        out_shape=(
            jax.ShapeDtypeStruct(loss.shape, f32), jax.ShapeDtypeStruct(grads.shape, f32)
        ),
        in_specs=[vmem] * 2,
        out_specs=(vmem, vmem),
    )(loss, grads)
    return (loss.reshape(-1), jnp.swapaxes(grads, 0, 1))


def solution(mesh):
    placed = (
        P("region", None, None),
        P("region", None, None),
        P("region", None),
        P(),
        P("region", None),
        P(),
        P(),
        P(),
        P(None, "region"),
    )
    return jax.shard_map(
        shards,
        mesh=mesh,
        in_specs=placed,
        out_specs=(P("region"), P("region", None, None)),
        check_vma=False,
    )
```
